512 devices in a mesh: ctx: 32 (over z, y_lo), tp: 16 (over x, y_hi, core).
Axes of the slice: x: 4, y: 8 (y_hi: 2, y_lo: 4; y = y_hi * 4 + y_lo), z: 8, core: 2. Of those that a mesh axis runs over, the one named last changes fastest.
Arguments:
- queries: bfloat16 [4096, 6144], P('ctx', 'tp'), may hold values from -6 to 6
- keys: bfloat16 [4096, 6144], P('ctx', 'tp'), may hold values from -6 to 6
- values: bfloat16 [4096, 6144], P('ctx', 'tp'), may hold values from -6 to 6
- norm_gain: float32 [6144], P('tp'), may hold values from 0.1 to 1.9
- out_weight: bfloat16 [6144, 6144], P('tp', 'ctx'), may hold values from -0.15625 to 0.15625
Outputs:
- projected: bfloat16 [4096, 6144], P('ctx', 'tp')
The draws below stay inside these ranges and needn't reach their ends.
All inputs are finite; a program needn't handle non-finite values.
Results may differ from the reference program's by a relative error of at most 0.017.
Values may be sent and summed in bfloat16 or wider, within the bound.
A program may use at most 64 MiB of HBM per device.

```python
import jax
import jax.numpy as jnp
from jax import lax

D = 6144
H = 48
HS = 128
TOK_DEV = 128
TOKENS = 4096
HD = 6144
N_CTX = 32
N_TP = 16


def spiked(drawn, rng, source, target, shards_of, factor):
    def block_of(axis_at):
        return (jnp.arange(drawn.shape[axis_at]) // (drawn.shape[axis_at] // shards_of)).reshape((-1,) + (1,) * (drawn.ndim - 1 - axis_at))

    first = jax.random.permutation(rng, shards_of)[block_of(target)]
    far = (block_of(target) + shards_of // 2) % shards_of
    return jnp.where((block_of(source) == first) | (block_of(source) == far), factor * drawn, drawn)


def steps_of(key, dims, split, low, high):
    gain = 1.0
    for dim, parts in split:
        steps = jax.random.uniform(jax.random.fold_in(jax.random.fold_in(key, 6), dim), (parts,), jnp.float32, low / len(split), high / len(split))
        gain = gain * jnp.repeat(jnp.exp(steps), dims[dim] // parts).reshape((-1,) + (1,) * (len(dims) - 1 - dim))
    return gain


def noise(rng, shape, scale, bound, pieces=(), held_as=jnp.bfloat16):
    drawn = scale * jax.random.normal(rng, shape, jnp.float32)
    if pieces:
        drawn = drawn * steps_of(rng, shape, pieces, -0.22, 0.18)
    return jnp.clip(drawn, -bound, bound).astype(held_as)


def bell_draw_with(stream_key, extent, spread, most, shards, heavy, kind=jnp.bfloat16):
    entries = spread * jax.random.normal(stream_key, extent, jnp.float32)
    if shards:
        entries = entries * steps_of(stream_key, extent, shards, -0.22, 0.18)
    return jnp.clip(spiked(entries, jax.random.fold_in(stream_key, 3), *heavy), -most, most).astype(kind)


def setup_inputs(seed: int = 0) -> dict:
    key_list = jax.random.split(jax.random.key(seed), 6)
    return {
        "queries": noise(key_list[0], (TOKENS, HD), 1.0, 6.0, ((0, 32), (1, 16))),
        "keys": noise(key_list[1], (TOKENS, HD), 1.0, 6.0, ((0, 32), (1, 16))),
        "values": noise(key_list[2], (TOKENS, HD), 1.0, 6.0, ((0, 32), (1, 16))),
        "norm_gain": jnp.clip(1.0 + 0.18 * jax.random.normal(key_list[3], (HD,), jnp.float32), 0.1, 1.9),
        "out_weight": bell_draw_with(key_list[4], (HD, D), HD ** -0.5, 0.15625, ((0, 16), (1, 32)), (0, 1, 32, 2.75)),
    }


def reference(queries, keys, values, norm_gain, out_weight):
    features = H * HS
    group_cols = features // N_TP
    gain_heads = norm_gain.reshape(H, HS)
    weight_groups = out_weight.reshape(N_TP, group_cols, D).astype(jnp.float32)
    causal = jnp.arange(TOK_DEV)[:, None] >= jnp.arange(TOK_DEV)[None, :]

    def advance(state_sum, blocks_in):
        query_rows, key_rows, value_rows = blocks_in
        query_heads = query_rows.reshape(TOK_DEV, H, HS).astype(jnp.float32)
        key_heads = key_rows.reshape(TOK_DEV, H, HS).astype(jnp.float32)
        value_heads = value_rows.reshape(TOK_DEV, H, HS).astype(jnp.float32)
        scores = jnp.einsum('thd,shd->hts', query_heads, key_heads, precision=lax.Precision.HIGHEST)
        scores = jnp.where(causal[None], scores, jnp.float32(0.0)).astype(jnp.bfloat16)
        scores = lax.optimization_barrier(scores).astype(jnp.float32)
        within = jnp.einsum('hts,shd->thd', scores, value_heads, precision=lax.Precision.HIGHEST)
        carried = jnp.einsum('thd,hde->the', query_heads, state_sum, precision=lax.Precision.HIGHEST)
        mixed_sum = within + carried
        inverse_rms = lax.rsqrt(lax.optimization_barrier(jnp.mean(mixed_sum * mixed_sum, axis=-1, keepdims=True)) + 1e-06)
        attended = (mixed_sum * inverse_rms * gain_heads).astype(jnp.bfloat16)
        attended = lax.optimization_barrier(attended).astype(jnp.float32)
        attended = attended.reshape(TOK_DEV, N_TP, group_cols)
        partials = jnp.einsum('tgc,gcd->gtd', attended, weight_groups, precision=lax.Precision.HIGHEST)
        partials = lax.optimization_barrier(partials.astype(jnp.bfloat16)).astype(jnp.float32)
        projected = lax.optimization_barrier(jnp.sum(partials, axis=0)).astype(jnp.bfloat16)
        local_state = jnp.einsum('shd,she->hde', key_heads, value_heads, precision=lax.Precision.HIGHEST)
        return (state_sum + local_state, projected)
    blocks_all = (queries.reshape(N_CTX, TOK_DEV, features), keys.reshape(N_CTX, TOK_DEV, features), values.reshape(N_CTX, TOK_DEV, features))
    start_state = jnp.zeros((H, HS, HS), jnp.float32)
    final_state, outputs = lax.scan(advance, start_state, blocks_all)
    return outputs.reshape(N_CTX * TOK_DEV, D)
```

```python
import jax
import jax.numpy as jnp
from jax import lax
from jax.experimental import pallas as pl
from jax.experimental.pallas import tpu as pltpu
from jax.sharding import PartitionSpec as P

HS = 128
HEADS = 3
F32 = jnp.float32
BF16 = jnp.bfloat16
MESH = pl.DeviceIdType.MESH


def remote(src, dst, send, recv, device):
    return pltpu.make_async_remote_copy(
        src_ref=src, dst_ref=dst, send_sem=send, recv_sem=recv, device_id=device, device_id_type=MESH
    )


class Ring:
    def __init__(self, buf, slot, pos, device, send, recv):
        self.buf, self.slot, self.pos, self.device = buf, slot, pos, device
        self.send, self.recv = send, recv
        self.half = buf.shape[1] // 2

    def copy(self, way, step, sub, back):
        origin = lax.rem(self.pos + (8 - back if way == 0 else back), 8)
        ref = self.buf.at[self.slot(origin), pl.ds(sub * self.half, self.half)]
        i = way * 8 + (step - 1) * 2 + sub
        return remote(ref, ref, self.send.at[i], self.recv.at[i], self.device(way))

    def subs(self, way, step):
        return (0, 1) if step < 4 else (way,)

    def start(self):
        for sub in (0, 1):
            for way in (0, 1):
                self.copy(way, 1, sub, 0).start()

    def hop(self, step):
        for sub in (0, 1):
            for way in (0, 1):
                if sub in self.subs(way, step):
                    self.copy(way, step, sub, step).wait_recv()
                    if step < 4 and sub in self.subs(way, step + 1):
                        self.copy(way, step + 1, sub, step).start()

    def finish(self):
        for step in (1, 2, 3, 4):
            for way in (0, 1):
                for sub in self.subs(way, step):
                    self.copy(way, step, sub, step - 1).wait_send()


def nt(a, b):
    return lax.dot_general(a, b, (((1,), (1,)), ((), ())), preferred_element_type=F32)


def kernel(
    q_ref, k_ref, v_ref, g_ref, w_ref, o_ref,
    sq, ra, tot, rb, base, pfx, rc, within, att, wst, wt, pc_out, pc_in, px_out, px_in, f_acc, f_out, f_in,
    s1, r1, s2, r2, s3, r3, s4, r4, ws, wr, as_, ar, cs, cr, xs, xr, fs, fr,
):
    c, g = lax.axis_index("ctx"), lax.axis_index("tp")
    z, yl = lax.div(c, 4), lax.rem(c, 4)
    x, yh, core = lax.div(g, 4), lax.rem(lax.div(g, 2), 2), lax.rem(g, 2)
    y = yh * 4 + yl

    def dev(z=z, yl=yl, x=x, yh=yh, core=core):
        return (z * 4 + yl, x * 4 + yh * 2 + core)

    def dev_y(yy):
        yy = lax.rem(yy, 8)
        return dev(yl=lax.rem(yy, 4), yh=lax.div(yy, 4))

    z_swap = z + 1 - 2 * lax.rem(z, 2)
    swap_dev = dev(z=z_swap, yh=1 - yh)
    peers = [dev(yl=lax.rem(yl + d, 4), core=lax.rem(core + e, 2)) for d in range(4) for e in range(2) if d + e]
    peers += [dev(z=lax.rem(z + d, 8)) for d in range(1, 8)]
    peers += [dev_y(y + 1), dev_y(y + 7)]
    peers += [dev(x=lax.rem(x + d, 4)) for d in range(1, 4)]
    peers += [swap_dev]
    barrier = pltpu.get_barrier_semaphore()
    for peer in peers:
        pl.semaphore_signal(barrier, inc=1, device_id=peer, device_id_type=MESH)

    for h in range(HEADS):
        cols = slice(h * HS, (h + 1) * HS)
        state = lax.dot_general(
            k_ref[:, cols], v_ref[:, cols], (((0,), (0,)), ((), ())), preferred_element_type=F32
        )
        sq[cols, :] = state.astype(BF16)
    pl.semaphore_wait(barrier, len(peers))

    def quarter(i):
        return pl.ds(pl.multiple_of(i * 96, 96), 96)

    def send1(d):
        to = lax.rem(yl + d, 4)
        return remote(sq.at[quarter(to)], ra.at[yl], s1.at[d - 1], r1.at[d - 1], dev(yl=to))

    for d in (1, 2, 3):
        send1(d).start()
    ra[yl] = sq[quarter(yl), :]

    def w_slot(s):
        return lax.rem(s, 2) * 4 + lax.div(s, 2)

    wst[...] = jnp.transpose(w_ref[...])
    same = lax.rem(z, 2) == yh
    swap = remote(wst, wt.at[w_slot(z_swap)], s4.at[0], r4.at[0], swap_dev)

    def recv1(d):
        frm = lax.rem(yl + 4 - d, 4)
        return remote(sq.at[quarter(yl)], ra.at[frm], s1.at[d - 1], r1.at[d - 1], dev(yl=frm))

    for d in (1, 2, 3):
        recv1(d).wait_recv()
    tot[...] = (
        (ra[0].astype(F32) + ra[1].astype(F32)) + (ra[2].astype(F32) + ra[3].astype(F32))
    ).astype(BF16)

    def copy2(d, to):
        return remote(tot, rb.at[d - 1], s2.at[d - 1], r2.at[d - 1], dev(z=to))

    for d in range(1, 8):
        @pl.when(z + d < 8)
        def _(d=d):
            copy2(d, lax.rem(z + d, 8)).start()

    @pl.when(jnp.logical_not(same))
    def _():
        swap.start()

    @pl.when(same)
    def _():
        wt[w_slot(z)] = wst[...]

    rows = lax.broadcasted_iota(jnp.int32, (HS, HS), 0)
    columns = lax.broadcasted_iota(jnp.int32, (HS, HS), 1)
    for h in range(HEADS):
        cols = slice(h * HS, (h + 1) * HS)
        scores = jnp.where(rows >= columns, nt(q_ref[:, cols], k_ref[:, cols]), 0.0).astype(BF16)
        within[:, cols] = jnp.dot(scores, v_ref[:, cols], preferred_element_type=F32)

    base[...] = jnp.zeros_like(base)
    for d in range(1, 8):
        @pl.when(z >= d)
        def _(d=d):
            copy2(d, lax.rem(z + 8 - d, 8)).wait_recv()
            base[...] += rb[d - 1].astype(F32)
    running = base[...]
    for i in range(4):
        pfx[i] = running.astype(BF16)
        if i < 3:
            running = running + ra[i].astype(F32)

    def send3(d):
        to = lax.rem(yl + d, 4)
        return remote(pfx.at[to], rc.at[quarter(yl)], s3.at[d - 1], r3.at[d - 1], dev(yl=to))

    for d in (1, 2, 3):
        send3(d).start()
    rc[quarter(yl), :] = pfx[yl]

    w_ring = Ring(wt, w_slot, z, lambda way: dev(z=lax.rem(z + (1 if way == 0 else 7), 8)), ws, wr)

    @pl.when(jnp.logical_not(same))
    def _():
        remote(wst, wt.at[w_slot(z)], s4.at[0], r4.at[0], swap_dev).wait_recv()

    w_ring.start()

    def recv3(d):
        frm = lax.rem(yl + 4 - d, 4)
        return remote(pfx.at[yl], rc.at[quarter(frm)], s3.at[d - 1], r3.at[d - 1], dev(yl=frm))

    for d in (1, 2, 3):
        recv3(d).wait_recv()

    for h in range(HEADS):
        cols = slice(h * HS, (h + 1) * HS)
        mixed = within[:, cols] + jnp.dot(q_ref[:, cols], rc[cols, :], preferred_element_type=F32)
        scale = lax.rsqrt(jnp.mean(mixed * mixed, axis=-1, keepdims=True) + 1e-06)
        att[y, :, cols] = (mixed * scale * g_ref[:, cols]).astype(BF16)

    a_ring = Ring(att, lambda s: s, y, lambda way: dev_y(y + (1 if way == 0 else 7)), as_, ar)
    a_ring.start()
    w_ring.hop(1)
    a_ring.hop(1)
    w_ring.hop(2)
    a_ring.hop(2)
    w_ring.hop(3)
    a_ring.hop(3)
    a_ring.hop(4)
    w_ring.hop(4)

    def tokens(p, half):
        return att[pl.ds(p * 4 + 2 * half, 2)].reshape(2 * HS, HEADS * HS)

    def unit(i, a):
        m = lax.rem(x + i, 4)
        return nt(wt[m], a[0]) + nt(wt[4 + m], a[1])

    partner = dev(core=1 - core)

    def copy_c(i):
        return remote(pc_out.at[i - 1], pc_in.at[i - 1], cs.at[i - 1], cr.at[i - 1], partner)

    theirs = (tokens(0, 1 - core), tokens(1, 1 - core))
    for i in (1, 2, 3, 4):
        pc_out[i - 1] = unit(i, theirs).astype(BF16)
        copy_c(i).start()

    def copy_x(i, to):
        return remote(px_out.at[i - 1], px_in.at[i - 1], xs.at[i - 1], xr.at[i - 1], dev(x=to))

    ours = (tokens(0, core), tokens(1, core))
    for i in (1, 2, 3, 4):
        mine = unit(i, ours)
        copy_c(i).wait_recv()
        mine = mine + pc_in[i - 1].astype(F32)
        if i < 4:
            px_out[i - 1] = mine.astype(BF16)
            copy_x(i, lax.rem(x + i, 4)).start()
        else:
            f_acc[...] = mine
    for i in (1, 2, 3):
        copy_x(i, lax.rem(x + 4 - i, 4)).wait_recv()
    total = f_acc[...] + px_in[0].astype(F32) + px_in[1].astype(F32) + px_in[2].astype(F32)

    f_out[0] = total[:, :HS].astype(BF16)
    f_out[1] = total[:, HS:].astype(BF16)
    half = lax.rem(yl, 2)

    def copy_f(i):
        return remote(
            f_out.at[i], f_in.at[half], fs.at[i], fr.at[half], dev(yl=2 * core + i, core=lax.div(yl, 2))
        )

    for i in (0, 1):
        @pl.when(2 * core + i != yl)
        def _(i=i):
            copy_f(i).start()

        @pl.when(2 * core + i == yl)
        def _(i=i):
            f_in[i] = f_out[i]

    for i in (0, 1):
        @pl.when(2 * core + i != yl)
        def _(i=i):
            remote(
                f_out.at[i], f_in.at[i], fs.at[i], fr.at[i], dev(yl=2 * core + i, core=lax.div(yl, 2))
            ).wait_recv()

    o_ref[...] = jnp.transpose(f_in[...].reshape(HEADS * HS, HS))

    for d in (1, 2, 3):
        send1(d).wait_send()
        send3(d).wait_send()
        copy_x(d, lax.rem(x + d, 4)).wait_send()
    for d in range(1, 8):
        @pl.when(z + d < 8)
        def _(d=d):
            copy2(d, lax.rem(z + d, 8)).wait_send()

    @pl.when(jnp.logical_not(same))
    def _():
        swap.wait_send()

    w_ring.finish()
    a_ring.finish()
    for i in (1, 2, 3, 4):
        copy_c(i).wait_send()
    for i in (0, 1):
        @pl.when(2 * core + i != yl)
        def _(i=i):
            copy_f(i).wait_send()


def body(queries, keys, values, norm_gain, out_weight):
    dma = [pltpu.SemaphoreType.DMA((n,)) for n in (3, 7, 3, 1, 16, 16, 4, 3, 2) for _ in (0, 1)]
    return pl.pallas_call(
        kernel,
        out_shape=jax.ShapeDtypeStruct((HS, HEADS * HS), BF16),
        in_specs=[pl.BlockSpec(memory_space=pltpu.VMEM)] * 5,
        out_specs=pl.BlockSpec(memory_space=pltpu.VMEM),
        scratch_shapes=[
            pltpu.VMEM((384, 128), BF16),
            pltpu.VMEM((4, 96, 128), BF16),
            pltpu.VMEM((96, 128), BF16),
            pltpu.VMEM((7, 96, 128), BF16),
            pltpu.VMEM((96, 128), F32),
            pltpu.VMEM((4, 96, 128), BF16),
            pltpu.VMEM((384, 128), BF16),
            pltpu.VMEM((128, 384), F32),
            pltpu.VMEM((8, 128, 384), BF16),
            pltpu.VMEM((192, 384), BF16),
            pltpu.VMEM((8, 192, 384), BF16),
            pltpu.VMEM((4, 192, 256), BF16),
            pltpu.VMEM((4, 192, 256), BF16),
            pltpu.VMEM((3, 192, 256), BF16),
            pltpu.VMEM((3, 192, 256), BF16),
            pltpu.VMEM((192, 256), F32),
            pltpu.VMEM((2, 192, 128), BF16),
            pltpu.VMEM((2, 192, 128), BF16),
        ] + dma,
        compiler_params=pltpu.CompilerParams(collective_id=0, has_side_effects=True),
    )(queries, keys, values, norm_gain.reshape(1, HEADS * HS), out_weight)


def solution(mesh):
    return jax.shard_map(
        body,
        mesh=mesh,
        in_specs=(P("ctx", "tp"), P("ctx", "tp"), P("ctx", "tp"), P("tp"), P("tp", "ctx")),
        out_specs=P("ctx", "tp"),
        check_vma=False,
    )
```

```python
import jax
import jax.numpy as jnp
from jax import lax
from jax.experimental import pallas as pl
from jax.experimental.pallas import tpu as pltpu
from jax.sharding import PartitionSpec as P

HS = 128
HEADS = 3
F32 = jnp.float32
BF16 = jnp.bfloat16
MESH = pl.DeviceIdType.MESH


def remote(src, dst, send, recv, device):
    return pltpu.make_async_remote_copy(
        src_ref=src, dst_ref=dst, send_sem=send, recv_sem=recv, device_id=device, device_id_type=MESH
    )


class Ring:
    def __init__(self, buf, slot, pos, device, send, recv):
        self.buf, self.slot, self.pos, self.device = buf, slot, pos, device
        self.send, self.recv = send, recv
        self.half = buf.shape[1] // 2

    def copy(self, way, step, sub, back):
        origin = lax.rem(self.pos + (8 - back if way == 0 else back), 8)
        ref = self.buf.at[self.slot(origin), pl.ds(sub * self.half, self.half)]
        i = way * 8 + (step - 1) * 2 + sub
        return remote(ref, ref, self.send.at[i], self.recv.at[i], self.device(way))

    def subs(self, way, step):
        return (0, 1) if step < 4 else (way,)

    def start(self):
        for sub in (0, 1):
            for way in (0, 1):
                self.copy(way, 1, sub, 0).start()

    def hop(self, step):
        for sub in (0, 1):
            for way in (0, 1):
                if sub in self.subs(way, step):
                    self.copy(way, step, sub, step).wait_recv()
                    if step < 4 and sub in self.subs(way, step + 1):
                        self.copy(way, step + 1, sub, step).start()

    def finish(self):
        for step in (1, 2, 3, 4):
            for way in (0, 1):
                for sub in self.subs(way, step):
                    self.copy(way, step, sub, step - 1).wait_send()


def nt(a, b):
    return lax.dot_general(a, b, (((1,), (1,)), ((), ())), preferred_element_type=F32)


def kernel(
    q_ref, k_ref, v_ref, g_ref, w_ref, o_ref,
    sq, ra, tot, rb, base, pfx, rc, within, att, wt, pc_out, pc_in, px_out, px_in, f_acc, f_out, f_in,
    s1, r1, s2, r2, s3, r3, s4, r4, ws, wr, as_, ar, cs, cr, xs, xr, fs, fr,
):
    c, g = lax.axis_index("ctx"), lax.axis_index("tp")
    z, yl = lax.div(c, 4), lax.rem(c, 4)
    x, yh, core = lax.div(g, 4), lax.rem(lax.div(g, 2), 2), lax.rem(g, 2)
    y = yh * 4 + yl

    def dev(z=z, yl=yl, x=x, yh=yh, core=core):
        return (z * 4 + yl, x * 4 + yh * 2 + core)

    def dev_y(yy):
        yy = lax.rem(yy, 8)
        return dev(yl=lax.rem(yy, 4), yh=lax.div(yy, 4))

    z_swap = z + 1 - 2 * lax.rem(z, 2)
    swap_dev = dev(z=z_swap, yh=1 - yh)
    peers = [dev(yl=lax.rem(yl + d, 4), core=lax.rem(core + e, 2)) for d in range(4) for e in range(2) if d + e]
    peers += [dev(z=lax.rem(z + d, 8)) for d in range(1, 8)]
    peers += [dev_y(y + 1), dev_y(y + 7)]
    peers += [dev(x=lax.rem(x + d, 4)) for d in range(1, 4)]
    peers += [swap_dev]
    barrier = pltpu.get_barrier_semaphore()
    for peer in peers:
        pl.semaphore_signal(barrier, inc=1, device_id=peer, device_id_type=MESH)

    for h in range(HEADS):
        cols = slice(h * HS, (h + 1) * HS)
        state = lax.dot_general(
            k_ref[:, cols], v_ref[:, cols], (((0,), (0,)), ((), ())), preferred_element_type=F32
        )
        sq[cols, :] = state.astype(BF16)
    pl.semaphore_wait(barrier, len(peers))

    def quarter(i):
        return pl.ds(pl.multiple_of(i * 96, 96), 96)

    def send1(d):
        to = lax.rem(yl + d, 4)
        return remote(sq.at[quarter(to)], ra.at[yl], s1.at[d - 1], r1.at[d - 1], dev(yl=to))

    for d in (1, 2, 3):
        send1(d).start()
    ra[yl] = sq[quarter(yl), :]

    def w_slot(s):
        return lax.rem(s, 2) * 4 + lax.div(s, 2)

    same = lax.rem(z, 2) == yh
    swap = remote(w_ref, wt.at[w_slot(z_swap)], s4.at[0], r4.at[0], swap_dev)

    @pl.when(jnp.logical_not(same))
    def _():
        swap.start()

    @pl.when(same)
    def _():
        wt[w_slot(z)] = w_ref[...]

    def recv1(d):
        frm = lax.rem(yl + 4 - d, 4)
        return remote(sq.at[quarter(yl)], ra.at[frm], s1.at[d - 1], r1.at[d - 1], dev(yl=frm))

    for d in (1, 2, 3):
        recv1(d).wait_recv()
    tot[...] = (
        (ra[0].astype(F32) + ra[1].astype(F32)) + (ra[2].astype(F32) + ra[3].astype(F32))
    ).astype(BF16)

    def copy2(d, to):
        return remote(tot, rb.at[d - 1], s2.at[d - 1], r2.at[d - 1], dev(z=to))

    for d in range(1, 8):
        @pl.when(z + d < 8)
        def _(d=d):
            copy2(d, lax.rem(z + d, 8)).start()

    rows = lax.broadcasted_iota(jnp.int32, (HS, HS), 0)
    columns = lax.broadcasted_iota(jnp.int32, (HS, HS), 1)
    for h in range(HEADS):
        cols = slice(h * HS, (h + 1) * HS)
        scores = jnp.where(rows >= columns, nt(q_ref[:, cols], k_ref[:, cols]), 0.0).astype(BF16)
        within[:, cols] = jnp.dot(scores, v_ref[:, cols], preferred_element_type=F32)

    base[...] = jnp.zeros_like(base)
    for d in range(1, 8):
        @pl.when(z >= d)
        def _(d=d):
            copy2(d, lax.rem(z + 8 - d, 8)).wait_recv()
            base[...] += rb[d - 1].astype(F32)
    running = base[...]
    for i in range(4):
        pfx[i] = running.astype(BF16)
        if i < 3:
            running = running + ra[i].astype(F32)

    def send3(d):
        to = lax.rem(yl + d, 4)
        return remote(pfx.at[to], rc.at[quarter(yl)], s3.at[d - 1], r3.at[d - 1], dev(yl=to))

    for d in (1, 2, 3):
        send3(d).start()
    rc[quarter(yl), :] = pfx[yl]

    w_ring = Ring(wt, w_slot, z, lambda way: dev(z=lax.rem(z + (1 if way == 0 else 7), 8)), ws, wr)

    @pl.when(jnp.logical_not(same))
    def _():
        remote(w_ref, wt.at[w_slot(z)], s4.at[0], r4.at[0], swap_dev).wait_recv()

    w_ring.start()

    def recv3(d):
        frm = lax.rem(yl + 4 - d, 4)
        return remote(pfx.at[yl], rc.at[quarter(frm)], s3.at[d - 1], r3.at[d - 1], dev(yl=frm))

    for d in (1, 2, 3):
        recv3(d).wait_recv()

    for h in range(HEADS):
        cols = slice(h * HS, (h + 1) * HS)
        mixed = within[:, cols] + jnp.dot(q_ref[:, cols], rc[cols, :], preferred_element_type=F32)
        scale = lax.rsqrt(jnp.mean(mixed * mixed, axis=-1, keepdims=True) + 1e-06)
        att[y, :, cols] = (mixed * scale * g_ref[cols]).astype(BF16)

    a_ring = Ring(att, lambda s: s, y, lambda way: dev_y(y + (1 if way == 0 else 7)), as_, ar)
    a_ring.start()
    w_ring.hop(1)
    a_ring.hop(1)
    w_ring.hop(2)
    a_ring.hop(2)
    w_ring.hop(3)
    a_ring.hop(3)
    a_ring.hop(4)
    w_ring.hop(4)

    def tokens(p, half):
        return att[pl.ds(p * 4 + 2 * half, 2)].reshape(2 * HS, HEADS * HS)

    def unit(i, a):
        m = lax.rem(x + i, 4)
        return nt(wt[m], a[0]) + nt(wt[4 + m], a[1])

    partner = dev(core=1 - core)

    def copy_c(i):
        return remote(pc_out.at[i - 1], pc_in.at[i - 1], cs.at[i - 1], cr.at[i - 1], partner)

    theirs = (tokens(0, 1 - core), tokens(1, 1 - core))
    for i in (1, 2, 3, 4):
        pc_out[i - 1] = unit(i, theirs).astype(BF16)
        copy_c(i).start()

    def copy_x(i, to):
        return remote(px_out.at[i - 1], px_in.at[i - 1], xs.at[i - 1], xr.at[i - 1], dev(x=to))

    ours = (tokens(0, core), tokens(1, core))
    for i in (1, 2, 3, 4):
        mine = unit(i, ours)
        copy_c(i).wait_recv()
        mine = mine + pc_in[i - 1].astype(F32)
        if i < 4:
            px_out[i - 1] = mine.astype(BF16)
            copy_x(i, lax.rem(x + i, 4)).start()
        else:
            f_acc[...] = mine
    for i in (1, 2, 3):
        copy_x(i, lax.rem(x + 4 - i, 4)).wait_recv()
    total = f_acc[...] + px_in[0].astype(F32) + px_in[1].astype(F32) + px_in[2].astype(F32)

    f_out[0] = total[:, :HS].astype(BF16)
    f_out[1] = total[:, HS:].astype(BF16)
    half = lax.rem(yl, 2)

    def copy_f(i):
        return remote(
            f_out.at[i], f_in.at[half], fs.at[i], fr.at[half], dev(yl=2 * core + i, core=lax.div(yl, 2))
        )

    for i in (0, 1):
        @pl.when(2 * core + i != yl)
        def _(i=i):
            copy_f(i).start()

        @pl.when(2 * core + i == yl)
        def _(i=i):
            f_in[i] = f_out[i]

    for i in (0, 1):
        @pl.when(2 * core + i != yl)
        def _(i=i):
            remote(
                f_out.at[i], f_in.at[i], fs.at[i], fr.at[i], dev(yl=2 * core + i, core=lax.div(yl, 2))
            ).wait_recv()

    o_ref[...] = jnp.transpose(f_in[...].reshape(HEADS * HS, HS))

    for d in (1, 2, 3):
        send1(d).wait_send()
        send3(d).wait_send()
        copy_x(d, lax.rem(x + d, 4)).wait_send()
    for d in range(1, 8):
        @pl.when(z + d < 8)
        def _(d=d):
            copy2(d, lax.rem(z + d, 8)).wait_send()

    @pl.when(jnp.logical_not(same))
    def _():
        swap.wait_send()

    w_ring.finish()
    a_ring.finish()
    for i in (1, 2, 3, 4):
        copy_c(i).wait_send()
    for i in (0, 1):
        @pl.when(2 * core + i != yl)
        def _(i=i):
            copy_f(i).wait_send()


def body(queries, keys, values, norm_gain, out_weight):
    dma = [pltpu.SemaphoreType.DMA((n,)) for n in (3, 7, 3, 1, 16, 16, 4, 3, 2) for _ in (0, 1)]
    return pl.pallas_call(
        kernel,
        out_shape=jax.ShapeDtypeStruct((HS, HEADS * HS), BF16),
        in_specs=[pl.BlockSpec(memory_space=pltpu.VMEM)] * 5,
        out_specs=pl.BlockSpec(memory_space=pltpu.VMEM),
        scratch_shapes=[
            pltpu.VMEM((384, 128), BF16),
            pltpu.VMEM((4, 96, 128), BF16),
            pltpu.VMEM((96, 128), BF16),
            pltpu.VMEM((7, 96, 128), BF16),
            pltpu.VMEM((96, 128), F32),
            pltpu.VMEM((4, 96, 128), BF16),
            pltpu.VMEM((384, 128), BF16),
            pltpu.VMEM((128, 384), F32),
            pltpu.VMEM((8, 128, 384), BF16),
            pltpu.VMEM((8, 192, 384), BF16),
            pltpu.VMEM((4, 192, 256), BF16),
            pltpu.VMEM((4, 192, 256), BF16),
            pltpu.VMEM((3, 192, 256), BF16),
            pltpu.VMEM((3, 192, 256), BF16),
            pltpu.VMEM((192, 256), F32),
            pltpu.VMEM((2, 192, 128), BF16),
            pltpu.VMEM((2, 192, 128), BF16),
        ] + dma,
        compiler_params=pltpu.CompilerParams(collective_id=0, has_side_effects=True),
    )(queries, keys, values, norm_gain, jnp.transpose(out_weight))


def solution(mesh):
    return jax.shard_map(
        body,
        mesh=mesh,
        in_specs=(P("ctx", "tp"), P("ctx", "tp"), P("ctx", "tp"), P("tp"), P("tp", "ctx")),
        out_specs=P("ctx", "tp"),
        check_vma=False,
    )
```

```python
import jax
import jax.numpy as jnp
from jax import lax
from jax.experimental import pallas as pl
from jax.experimental.pallas import tpu as pltpu
from jax.sharding import PartitionSpec as P

HS = 128
HEADS = 3
F32 = jnp.float32
BF16 = jnp.bfloat16
MESH = pl.DeviceIdType.MESH


def remote(src, dst, send, recv, device):
    return pltpu.make_async_remote_copy(
        src_ref=src, dst_ref=dst, send_sem=send, recv_sem=recv, device_id=device, device_id_type=MESH
    )


class Ring:
    def __init__(self, buf, slot, pos, device, send, recv):
        self.buf, self.slot, self.pos, self.device = buf, slot, pos, device
        self.send, self.recv = send, recv
        self.half = buf.shape[1] // 2

    def copy(self, way, step, sub, back):
        origin = lax.rem(self.pos + (8 - back if way == 0 else back), 8)
        ref = self.buf.at[self.slot(origin), pl.ds(sub * self.half, self.half)]
        i = way * 8 + (step - 1) * 2 + sub
        return remote(ref, ref, self.send.at[i], self.recv.at[i], self.device(way))

    def subs(self, way, step):
        return (0, 1) if step < 4 else (way,)

    def start(self):
        for sub in (0, 1):
            for way in (0, 1):
                self.copy(way, 1, sub, 0).start()

    def hop(self, step):
        for sub in (0, 1):
            for way in (0, 1):
                if sub in self.subs(way, step):
                    self.copy(way, step, sub, step).wait_recv()
                    if step < 4 and sub in self.subs(way, step + 1):
                        self.copy(way, step + 1, sub, step).start()

    def finish(self):
        for step in (1, 2, 3, 4):
            for way in (0, 1):
                for sub in self.subs(way, step):
                    self.copy(way, step, sub, step - 1).wait_send()


class Line:
    def __init__(self, buf, pos, device, send, recv):
        self.buf, self.pos, self.device, self.send, self.recv = buf, pos, device, send, recv
        self.half = buf.shape[1] // 2

    def copy(self, way, step, sub, back):
        origin = lax.rem(self.pos + (4 - back if way == 0 else back), 4)
        ref = self.buf.at[origin, pl.ds(sub * self.half, self.half)]
        i = way * 6 + (step - 1) * 2 + sub
        return remote(ref, ref, self.send.at[i], self.recv.at[i], self.device(way))

    def room(self, way):
        return self.pos if way == 0 else 3 - self.pos

    def sends(self, way, step):
        return jnp.logical_and(self.room(way) < 3, self.room(way) >= step - 1)

    def start(self):
        for sub in (0, 1):
            for way in (0, 1):
                @pl.when(self.sends(way, 1))
                def _():
                    self.copy(way, 1, sub, 0).start()

    def hop(self, step):
        for sub in (0, 1):
            for way in (0, 1):
                @pl.when(self.room(way) >= step)
                def _():
                    self.copy(way, step, sub, step).wait_recv()
                if step < 3:
                    @pl.when(self.sends(way, step + 1))
                    def _():
                        self.copy(way, step + 1, sub, step).start()

    def finish(self):
        for step in (1, 2, 3):
            for way in (0, 1):
                for sub in (0, 1):
                    @pl.when(self.sends(way, step))
                    def _():
                        self.copy(way, step, sub, step - 1).wait_send()


def nt(a, b):
    return lax.dot_general(a, b, (((1,), (1,)), ((), ())), preferred_element_type=F32)


def kernel(
    q_ref, k_ref, v_ref, g_ref, w_ref, o_ref,
    sq, ra, tot, rb, base, pfx, rc, within, att, wt, pc_out, pc_in, px_out, px_in, f_acc, f_out, f_in,
    s1, r1, s2, r2, s3, r3, ws, wr, as_, ar, cs, cr, xs, xr, fs, fr,
):
    c, g = lax.axis_index("ctx"), lax.axis_index("tp")
    z, yl = lax.div(c, 4), lax.rem(c, 4)
    x, yh, core = lax.div(g, 4), lax.rem(lax.div(g, 2), 2), lax.rem(g, 2)

    def dev(z=z, yl=yl, x=x, yh=yh, core=core):
        return (z * 4 + yl, x * 4 + yh * 2 + core)

    peers = [dev(yl=lax.rem(yl + d, 4), core=lax.rem(core + e, 2)) for d in range(4) for e in range(2) if d + e]
    peers += [dev(z=lax.rem(z + d, 8)) for d in range(1, 8)]
    peers += [dev(yl=2 * core + i, yh=1 - yh, core=lax.div(yl, 2)) for i in range(2)]
    peers += [dev(x=lax.rem(x + d, 4)) for d in range(1, 4)]
    barrier = pltpu.get_barrier_semaphore()
    for peer in peers:
        pl.semaphore_signal(barrier, inc=1, device_id=peer, device_id_type=MESH)

    for h in range(HEADS):
        cols = slice(h * HS, (h + 1) * HS)
        state = lax.dot_general(
            k_ref[:, cols], v_ref[:, cols], (((0,), (0,)), ((), ())), preferred_element_type=F32
        )
        sq[cols, :] = state.astype(BF16)
    pl.semaphore_wait(barrier, len(peers))

    def quarter(i):
        return pl.ds(pl.multiple_of(i * 96, 96), 96)

    def send1(d):
        to = lax.rem(yl + d, 4)
        return remote(sq.at[quarter(to)], ra.at[yl], s1.at[d - 1], r1.at[d - 1], dev(yl=to))

    for d in (1, 2, 3):
        send1(d).start()
    ra[yl] = sq[quarter(yl), :]

    wt[z] = w_ref[...]
    w_ring = Ring(wt, lambda o: o, z, lambda way: dev(z=lax.rem(z + (1 if way == 0 else 7), 8)), ws, wr)

    w_ring.start()

    def recv1(d):
        frm = lax.rem(yl + 4 - d, 4)
        return remote(sq.at[quarter(yl)], ra.at[frm], s1.at[d - 1], r1.at[d - 1], dev(yl=frm))

    for d in (1, 2, 3):
        recv1(d).wait_recv()
    tot[...] = (
        (ra[0].astype(F32) + ra[1].astype(F32)) + (ra[2].astype(F32) + ra[3].astype(F32))
    ).astype(BF16)

    def copy2(d, to):
        return remote(tot, rb.at[d - 1], s2.at[d - 1], r2.at[d - 1], dev(z=to))

    for d in range(1, 8):
        @pl.when(z + d < 8)
        def _(d=d):
            copy2(d, lax.rem(z + d, 8)).start()

    rows = lax.broadcasted_iota(jnp.int32, (HS, HS), 0)
    columns = lax.broadcasted_iota(jnp.int32, (HS, HS), 1)
    for h in range(HEADS):
        cols = slice(h * HS, (h + 1) * HS)
        scores = jnp.where(rows >= columns, nt(q_ref[:, cols], k_ref[:, cols]), 0.0).astype(BF16)
        within[:, cols] = jnp.dot(scores, v_ref[:, cols], preferred_element_type=F32)

    w_ring.hop(1)
    base[...] = jnp.zeros_like(base)
    for d in range(1, 8):
        @pl.when(z >= d)
        def _(d=d):
            copy2(d, lax.rem(z + 8 - d, 8)).wait_recv()
            base[...] += rb[d - 1].astype(F32)
    running = base[...]
    for i in range(4):
        pfx[i] = running.astype(BF16)
        if i < 3:
            running = running + ra[i].astype(F32)

    def send3(d):
        to = lax.rem(yl + d, 4)
        return remote(pfx.at[to], rc.at[quarter(yl)], s3.at[d - 1], r3.at[d - 1], dev(yl=to))

    for d in (1, 2, 3):
        send3(d).start()
    rc[quarter(yl), :] = pfx[yl]

    w_ring.hop(2)

    def recv3(d):
        frm = lax.rem(yl + 4 - d, 4)
        return remote(pfx.at[yl], rc.at[quarter(frm)], s3.at[d - 1], r3.at[d - 1], dev(yl=frm))

    for d in (1, 2, 3):
        recv3(d).wait_recv()

    for h in range(HEADS):
        cols = slice(h * HS, (h + 1) * HS)
        mixed = within[:, cols] + jnp.dot(q_ref[:, cols], rc[cols, :], preferred_element_type=F32)
        scale = lax.rsqrt(jnp.mean(mixed * mixed, axis=-1, keepdims=True) + 1e-06)
        att[yl, :, cols] = (mixed * scale * g_ref[cols]).astype(BF16)

    a_line = Line(att, yl, lambda way: dev(yl=lax.rem(yl + (1 if way == 0 else 3), 4)), as_, ar)
    a_line.start()
    w_ring.hop(3)
    a_line.hop(1)
    a_line.hop(2)
    w_ring.hop(4)
    a_line.hop(3)

    def tokens(half):
        return att[pl.ds(2 * half, 2)].reshape(2 * HS, HEADS * HS)

    def unit(i, a):
        return nt(wt[pl.ds(2 * lax.rem(x + i, 4), 2)].reshape(2 * 192, HEADS * HS), a)

    partner = dev(core=1 - core)

    def copy_c(i):
        return remote(pc_out.at[i - 1], pc_in.at[i - 1], cs.at[i - 1], cr.at[i - 1], partner)

    def copy_x(i, to):
        return remote(px_out.at[i - 1], px_in.at[i - 1], xs.at[i - 1], xr.at[i - 1], dev(x=to))

    theirs, ours = tokens(1 - core), tokens(core)

    def give(i):
        pc_out[i - 1] = unit(i, theirs).astype(BF16)
        copy_c(i).start()

    order = (2, 1, 3, 4)
    give(order[0])
    for n, i in enumerate(order):
        if i < 4:
            give(order[n + 1])
        mine = unit(i, ours)
        copy_c(i).wait_recv()
        mine = mine + pc_in[i - 1].astype(F32)
        if i < 4:
            px_out[i - 1] = mine.astype(BF16)
            copy_x(i, lax.rem(x + i, 4)).start()
        else:
            f_acc[...] = mine
    for i in (1, 2, 3):
        copy_x(i, lax.rem(x + 4 - i, 4)).wait_recv()
    total = f_acc[...] + px_in[0].astype(F32) + px_in[1].astype(F32) + px_in[2].astype(F32)

    f_acc[...] = total
    half = lax.rem(yl, 2)

    def copy_f(e, i, slot):
        to = dev(yl=2 * core + i, yh=lax.rem(yh + e, 2), core=lax.div(yl, 2))
        return remote(f_out.at[e * 2 + i], f_in.at[e * 2 + slot], fs.at[e * 2 + i], fr.at[e * 2 + slot], to)

    def each_f(act):
        for e in (1, 0):
            for i in (0, 1):
                if e:
                    act(e, i)
                else:
                    pl.when(2 * core + i != yl)(lambda e=e, i=i: act(e, i))

    for e in (1, 0):
        part = f_acc[pl.ds(pl.multiple_of(lax.rem(yh + e, 2) * 192, 192), 192), :]
        f_out[e * 2] = part[:, :HS].astype(BF16)
        f_out[e * 2 + 1] = part[:, HS:].astype(BF16)
    each_f(lambda e, i: copy_f(e, i, half).start())
    for i in (0, 1):
        @pl.when(2 * core + i == yl)
        def _(i=i):
            f_in[i] = f_out[i]
    each_f(lambda e, i: copy_f(e, i, i).wait_recv())

    same = f_in[0:2].reshape(HEADS * HS, HS).astype(F32)
    other = f_in[2:4].reshape(HEADS * HS, HS).astype(F32)
    o_ref[...] = jnp.transpose((same + other).astype(BF16))

    for d in (1, 2, 3):
        send1(d).wait_send()
        send3(d).wait_send()
        copy_x(d, lax.rem(x + d, 4)).wait_send()
    for d in range(1, 8):
        @pl.when(z + d < 8)
        def _(d=d):
            copy2(d, lax.rem(z + d, 8)).wait_send()

    w_ring.finish()
    a_line.finish()
    for i in (1, 2, 3, 4):
        copy_c(i).wait_send()
    each_f(lambda e, i: copy_f(e, i, half).wait_send())


def body(queries, keys, values, norm_gain, out_weight):
    dma = [pltpu.SemaphoreType.DMA((n,)) for n in (3, 7, 3, 16, 12, 4, 3, 4) for _ in (0, 1)]
    return pl.pallas_call(
        kernel,
        out_shape=jax.ShapeDtypeStruct((HS, HEADS * HS), BF16),
        in_specs=[pl.BlockSpec(memory_space=pltpu.VMEM)] * 5,
        out_specs=pl.BlockSpec(memory_space=pltpu.VMEM),
        scratch_shapes=[
            pltpu.VMEM((384, 128), BF16),
            pltpu.VMEM((4, 96, 128), BF16),
            pltpu.VMEM((96, 128), BF16),
            pltpu.VMEM((7, 96, 128), BF16),
            pltpu.VMEM((96, 128), F32),
            pltpu.VMEM((4, 96, 128), BF16),
            pltpu.VMEM((384, 128), BF16),
            pltpu.VMEM((128, 384), F32),
            pltpu.VMEM((4, 128, 384), BF16),
            pltpu.VMEM((8, 192, 384), BF16),
            pltpu.VMEM((4, 384, 256), BF16),
            pltpu.VMEM((4, 384, 256), BF16),
            pltpu.VMEM((3, 384, 256), BF16),
            pltpu.VMEM((3, 384, 256), BF16),
            pltpu.VMEM((384, 256), F32),
            pltpu.VMEM((4, 192, 128), BF16),
            pltpu.VMEM((4, 192, 128), BF16),
        ] + dma,
        compiler_params=pltpu.CompilerParams(collective_id=0, has_side_effects=True),
    )(queries, keys, values, norm_gain, jnp.transpose(out_weight))


def solution(mesh):
    return jax.shard_map(
        body,
        mesh=mesh,
        in_specs=(P("ctx", "tp"), P("ctx", "tp"), P("ctx", "tp"), P("tp"), P("tp", "ctx")),
        out_specs=P("ctx", "tp"),
        check_vma=False,
    )
```

```python
import jax
import jax.numpy as jnp
from jax import lax
from jax.experimental import pallas as pl
from jax.experimental.pallas import tpu as pltpu
from jax.sharding import PartitionSpec as P

HS = 128
HEADS = 3
F32 = jnp.float32
BF16 = jnp.bfloat16
MESH = pl.DeviceIdType.MESH


def remote(src, dst, send, recv, device):
    return pltpu.make_async_remote_copy(
        src_ref=src, dst_ref=dst, send_sem=send, recv_sem=recv, device_id=device, device_id_type=MESH
    )


class Ring:
    def __init__(self, buf, slot, pos, device, send, recv):
        self.buf, self.slot, self.pos, self.device = buf, slot, pos, device
        self.send, self.recv = send, recv
        self.half = buf.shape[1] // 2

    def copy(self, way, step, sub, back):
        origin = lax.rem(self.pos + (8 - back if way == 0 else back), 8)
        ref = self.buf.at[self.slot(origin), pl.ds(sub * self.half, self.half)]
        i = way * 8 + (step - 1) * 2 + sub
        return remote(ref, ref, self.send.at[i], self.recv.at[i], self.device(way))

    def subs(self, way, step):
        return (0, 1) if step < 4 else (way,)

    def start(self):
        for sub in (0, 1):
            for way in (0, 1):
                self.copy(way, 1, sub, 0).start()

    def hop(self, step):
        for sub in (0, 1):
            for way in (0, 1):
                if sub in self.subs(way, step):
                    self.copy(way, step, sub, step).wait_recv()
                    if step < 4 and sub in self.subs(way, step + 1):
                        self.copy(way, step + 1, sub, step).start()

    def finish(self):
        for step in (1, 2, 3, 4):
            for way in (0, 1):
                for sub in self.subs(way, step):
                    self.copy(way, step, sub, step - 1).wait_send()


class Line:
    def __init__(self, buf, pos, device, send, recv):
        self.buf, self.pos, self.device, self.send, self.recv = buf, pos, device, send, recv
        self.half = buf.shape[1] // 2

    def copy(self, way, step, sub, back):
        origin = lax.rem(self.pos + (4 - back if way == 0 else back), 4)
        ref = self.buf.at[origin, pl.ds(sub * self.half, self.half)]
        i = way * 6 + (step - 1) * 2 + sub
        return remote(ref, ref, self.send.at[i], self.recv.at[i], self.device(way))

    def room(self, way):
        return self.pos if way == 0 else 3 - self.pos

    def sends(self, way, step):
        return jnp.logical_and(self.room(way) < 3, self.room(way) >= step - 1)

    def start(self):
        for sub in (0, 1):
            for way in (0, 1):
                @pl.when(self.sends(way, 1))
                def _():
                    self.copy(way, 1, sub, 0).start()

    def hop(self, step):
        for sub in (0, 1):
            for way in (0, 1):
                @pl.when(self.room(way) >= step)
                def _():
                    self.copy(way, step, sub, step).wait_recv()
                if step < 3:
                    @pl.when(self.sends(way, step + 1))
                    def _():
                        self.copy(way, step + 1, sub, step).start()

    def finish(self):
        for step in (1, 2, 3):
            for way in (0, 1):
                for sub in (0, 1):
                    @pl.when(self.sends(way, step))
                    def _():
                        self.copy(way, step, sub, step - 1).wait_send()


def nt(a, b):
    return lax.dot_general(a, b, (((1,), (1,)), ((), ())), preferred_element_type=F32)


def kernel(
    q_ref, k_ref, v_ref, g_ref, w_ref, o_ref,
    sq, ra, tot, rb, base, pfx, rc, within, att, wt, pc_out, pc_in, px_out, px_in, f_acc, f_out, f_in,
    s1, r1, s2, r2, s3, r3, ws, wr, as_, ar, cs, cr, xs, xr, fs, fr,
):
    c, g = lax.axis_index("ctx"), lax.axis_index("tp")
    z, yl = lax.div(c, 4), lax.rem(c, 4)
    x, yh, core = lax.div(g, 4), lax.rem(lax.div(g, 2), 2), lax.rem(g, 2)

    def dev(z=z, yl=yl, x=x, yh=yh, core=core):
        return (z * 4 + yl, x * 4 + yh * 2 + core)

    peers = [dev(yl=lax.rem(yl + d, 4), core=lax.rem(core + e, 2)) for d in range(4) for e in range(2) if d + e]
    peers += [dev(z=lax.rem(z + d, 8)) for d in range(1, 8)]
    peers += [dev(yl=2 * core + i, yh=1 - yh, core=lax.div(yl, 2)) for i in range(2)]
    peers += [dev(x=lax.rem(x + d, 4)) for d in range(1, 4)]
    barrier = pltpu.get_barrier_semaphore()
    for peer in peers:
        pl.semaphore_signal(barrier, inc=1, device_id=peer, device_id_type=MESH)

    for h in range(HEADS):
        cols = slice(h * HS, (h + 1) * HS)
        state = lax.dot_general(
            k_ref[:, cols], v_ref[:, cols], (((0,), (0,)), ((), ())), preferred_element_type=F32
        )
        sq[cols, :] = state.astype(BF16)
    pl.semaphore_wait(barrier, len(peers))

    def quarter(i):
        return pl.ds(pl.multiple_of(i * 96, 96), 96)

    def send1(d):
        to = lax.rem(yl + d, 4)
        return remote(sq.at[quarter(to)], ra.at[yl], s1.at[d - 1], r1.at[d - 1], dev(yl=to))

    for d in (1, 2, 3):
        send1(d).start()
    ra[yl] = sq[quarter(yl), :]

    wt[z] = w_ref[...]
    w_ring = Ring(wt, lambda o: o, z, lambda way: dev(z=lax.rem(z + (1 if way == 0 else 7), 8)), ws, wr)

    w_ring.start()

    def recv1(d):
        frm = lax.rem(yl + 4 - d, 4)
        return remote(sq.at[quarter(yl)], ra.at[frm], s1.at[d - 1], r1.at[d - 1], dev(yl=frm))

    for d in (1, 2, 3):
        recv1(d).wait_recv()
    tot[...] = (
        (ra[0].astype(F32) + ra[1].astype(F32)) + (ra[2].astype(F32) + ra[3].astype(F32))
    ).astype(BF16)

    def copy2(d, to):
        return remote(tot, rb.at[d - 1], s2.at[d - 1], r2.at[d - 1], dev(z=to))

    for d in range(1, 8):
        @pl.when(z + d < 8)
        def _(d=d):
            copy2(d, lax.rem(z + d, 8)).start()

    rows = lax.broadcasted_iota(jnp.int32, (HS, HS), 0)
    columns = lax.broadcasted_iota(jnp.int32, (HS, HS), 1)
    for h in range(HEADS):
        cols = slice(h * HS, (h + 1) * HS)
        scores = jnp.where(rows >= columns, nt(q_ref[:, cols], k_ref[:, cols]), 0.0).astype(BF16)
        within[:, cols] = jnp.dot(scores, v_ref[:, cols], preferred_element_type=F32)

    w_ring.hop(1)
    base[...] = jnp.zeros_like(base)
    for d in range(1, 8):
        @pl.when(z >= d)
        def _(d=d):
            copy2(d, lax.rem(z + 8 - d, 8)).wait_recv()
            base[...] += rb[d - 1].astype(F32)
    running = base[...]
    for i in range(4):
        pfx[i] = running.astype(BF16)
        if i < 3:
            running = running + ra[i].astype(F32)

    def send3(d):
        to = lax.rem(yl + d, 4)
        return remote(pfx.at[to], rc.at[quarter(yl)], s3.at[d - 1], r3.at[d - 1], dev(yl=to))

    for d in (1, 2, 3):
        send3(d).start()
    rc[quarter(yl), :] = pfx[yl]

    w_ring.hop(2)

    def recv3(d):
        frm = lax.rem(yl + 4 - d, 4)
        return remote(pfx.at[yl], rc.at[quarter(frm)], s3.at[d - 1], r3.at[d - 1], dev(yl=frm))

    for d in (1, 2, 3):
        recv3(d).wait_recv()

    for h in range(HEADS):
        cols = slice(h * HS, (h + 1) * HS)
        mixed = within[:, cols] + jnp.dot(q_ref[:, cols], rc[cols, :], preferred_element_type=F32)
        scale = lax.rsqrt(jnp.mean(mixed * mixed, axis=-1, keepdims=True) + 1e-06)
        att[yl, :, cols] = (mixed * scale * g_ref[cols]).astype(BF16)

    a_line = Line(att, yl, lambda way: dev(yl=lax.rem(yl + (1 if way == 0 else 3), 4)), as_, ar)
    a_line.start()
    w_ring.hop(3)
    a_line.hop(1)
    a_line.hop(2)
    w_ring.hop(4)
    a_line.hop(3)

    def tokens(half):
        return att[pl.ds(2 * half, 2)].reshape(2 * HS, HEADS * HS)

    def unit(e, i, a):
        return nt(wt[2 * lax.rem(x + i, 4) + lax.rem(yh + e, 2)], a)

    partner = dev(core=1 - core)

    def copy_c(e, i):
        n = e * 4 + i - 1
        return remote(pc_out.at[n], pc_in.at[n], cs.at[n], cr.at[n], partner)

    def copy_x(e, i, to):
        n = e * 3 + i - 1
        return remote(px_out.at[n], px_in.at[n], xs.at[n], xr.at[n], dev(x=to))

    theirs, ours = tokens(1 - core), tokens(core)

    def give(e, i):
        pc_out[e * 4 + i - 1] = unit(e, i, theirs).astype(BF16)
        copy_c(e, i).start()

    order = [(e, i) for e in (1, 0) for i in (2, 1, 3, 4)]
    give(*order[0])
    for n, (e, i) in enumerate(order):
        if n < 7:
            give(*order[n + 1])
        mine = unit(e, i, ours)
        copy_c(e, i).wait_recv()
        mine = mine + pc_in[e * 4 + i - 1].astype(F32)
        if i < 4:
            px_out[e * 3 + i - 1] = mine.astype(BF16)
            copy_x(e, i, lax.rem(x + i, 4)).start()
        else:
            f_acc[e] = mine

    half = lax.rem(yl, 2)

    def copy_f(e, i, slot):
        to = dev(yl=2 * core + i, yh=lax.rem(yh + e, 2), core=lax.div(yl, 2))
        return remote(f_out.at[e * 2 + i], f_in.at[e * 2 + slot], fs.at[e * 2 + i], fr.at[e * 2 + slot], to)

    def each_f(act, es=(1, 0)):
        for e in es:
            for i in (0, 1):
                if e:
                    act(e, i)
                else:
                    pl.when(2 * core + i != yl)(lambda e=e, i=i: act(e, i))

    for e in (1, 0):
        for i in (1, 2, 3):
            copy_x(e, i, lax.rem(x + 4 - i, 4)).wait_recv()
        total = f_acc[e]
        for i in (1, 2, 3):
            total = total + px_in[e * 3 + i - 1].astype(F32)
        f_out[e * 2] = total[:, :HS].astype(BF16)
        f_out[e * 2 + 1] = total[:, HS:].astype(BF16)
        each_f(lambda e, i: copy_f(e, i, half).start(), (e,))
    for i in (0, 1):
        @pl.when(2 * core + i == yl)
        def _(i=i):
            f_in[i] = f_out[i]
    each_f(lambda e, i: copy_f(e, i, i).wait_recv())

    same = f_in[0:2].reshape(HEADS * HS, HS).astype(F32)
    other = f_in[2:4].reshape(HEADS * HS, HS).astype(F32)
    o_ref[...] = jnp.transpose((same + other).astype(BF16))

    for d in (1, 2, 3):
        send1(d).wait_send()
        send3(d).wait_send()
        copy_x(0, d, lax.rem(x + d, 4)).wait_send()
        copy_x(1, d, lax.rem(x + d, 4)).wait_send()
    for d in range(1, 8):
        @pl.when(z + d < 8)
        def _(d=d):
            copy2(d, lax.rem(z + d, 8)).wait_send()

    w_ring.finish()
    a_line.finish()
    for i in (1, 2, 3, 4):
        copy_c(0, i).wait_send()
        copy_c(1, i).wait_send()
    each_f(lambda e, i: copy_f(e, i, half).wait_send())


def body(queries, keys, values, norm_gain, out_weight):
    dma = [pltpu.SemaphoreType.DMA((n,)) for n in (3, 7, 3, 16, 12, 8, 6, 4) for _ in (0, 1)]
    return pl.pallas_call(
        kernel,
        out_shape=jax.ShapeDtypeStruct((HS, HEADS * HS), BF16),
        in_specs=[pl.BlockSpec(memory_space=pltpu.VMEM)] * 5,
        out_specs=pl.BlockSpec(memory_space=pltpu.VMEM),
        scratch_shapes=[
            pltpu.VMEM((384, 128), BF16),
            pltpu.VMEM((4, 96, 128), BF16),
            pltpu.VMEM((96, 128), BF16),
            pltpu.VMEM((7, 96, 128), BF16),
            pltpu.VMEM((96, 128), F32),
            pltpu.VMEM((4, 96, 128), BF16),
            pltpu.VMEM((384, 128), BF16),
            pltpu.VMEM((128, 384), F32),
            pltpu.VMEM((4, 128, 384), BF16),
            pltpu.VMEM((8, 192, 384), BF16),
            pltpu.VMEM((8, 192, 256), BF16),
            pltpu.VMEM((8, 192, 256), BF16),
            pltpu.VMEM((6, 192, 256), BF16),
            pltpu.VMEM((6, 192, 256), BF16),
            pltpu.VMEM((2, 192, 256), F32),
            pltpu.VMEM((4, 192, 128), BF16),
            pltpu.VMEM((4, 192, 128), BF16),
        ] + dma,
        compiler_params=pltpu.CompilerParams(collective_id=0, has_side_effects=True),
    )(queries, keys, values, norm_gain, jnp.transpose(out_weight))


def solution(mesh):
    return jax.shard_map(
        body,
        mesh=mesh,
        in_specs=(P("ctx", "tp"), P("ctx", "tp"), P("ctx", "tp"), P("tp"), P("tp", "ctx")),
        out_specs=P("ctx", "tp"),
        check_vma=False,
    )
```

```python
import jax
import jax.numpy as jnp
from jax import lax
from jax.experimental import pallas as pl
from jax.experimental.pallas import tpu as pltpu
from jax.sharding import PartitionSpec as P

HS = 128
HEADS = 3
F32 = jnp.float32
BF16 = jnp.bfloat16
MESH = pl.DeviceIdType.MESH


def remote(src, dst, send, recv, device):
    return pltpu.make_async_remote_copy(
        src_ref=src, dst_ref=dst, send_sem=send, recv_sem=recv, device_id=device, device_id_type=MESH
    )


class Ring:
    def __init__(self, buf, slot, pos, device, send, recv):
        self.buf, self.slot, self.pos, self.device = buf, slot, pos, device
        self.send, self.recv = send, recv
        self.half = buf.shape[1] // 2

    def copy(self, way, step, sub, back):
        origin = lax.rem(self.pos + (8 - back if way == 0 else back), 8)
        ref = self.buf.at[self.slot(origin), pl.ds(sub * self.half, self.half)]
        i = way * 8 + (step - 1) * 2 + sub
        return remote(ref, ref, self.send.at[i], self.recv.at[i], self.device(way))

    def subs(self, way, step):
        return (0, 1) if step < 4 else (way,)

    def start(self):
        for sub in (0, 1):
            for way in (0, 1):
                self.copy(way, 1, sub, 0).start()

    def hop(self, step):
        for sub in (0, 1):
            for way in (0, 1):
                if sub in self.subs(way, step):
                    self.copy(way, step, sub, step).wait_recv()
                    if step < 4 and sub in self.subs(way, step + 1):
                        self.copy(way, step + 1, sub, step).start()

    def finish(self):
        for step in (1, 2, 3, 4):
            for way in (0, 1):
                for sub in self.subs(way, step):
                    self.copy(way, step, sub, step - 1).wait_send()


def nt(a, b):
    return lax.dot_general(a, b, (((1,), (1,)), ((), ())), preferred_element_type=F32)


def kernel(
    q_ref, k_ref, v_ref, g_ref, w_ref, o_ref,
    sq, ra, tot, rb, base, pfx, rc, within, att, wt, pc_out, pc_in, px_out, px_in, f_acc, f_out, f_in,
    s1, r1, s2, r2, s3, r3, ws, wr, as_, ar, cs, cr, xs, xr, fs, fr,
):
    c, g = lax.axis_index("ctx"), lax.axis_index("tp")
    z, yl = lax.div(c, 4), lax.rem(c, 4)
    x, yh, core = lax.div(g, 4), lax.rem(lax.div(g, 2), 2), lax.rem(g, 2)

    def dev(z=z, yl=yl, x=x, yh=yh, core=core):
        return (z * 4 + yl, x * 4 + yh * 2 + core)

    peers = [dev(yl=lax.rem(yl + d, 4), core=lax.rem(core + e, 2)) for d in range(4) for e in range(2) if d + e]
    peers += [dev(z=lax.rem(z + d, 8)) for d in range(1, 8)]
    peers += [dev(yl=2 * core + i, yh=1 - yh, core=lax.div(yl, 2)) for i in range(2)]
    peers += [dev(x=lax.rem(x + d, 4)) for d in range(1, 4)]
    barrier = pltpu.get_barrier_semaphore()
    for peer in peers:
        pl.semaphore_signal(barrier, inc=1, device_id=peer, device_id_type=MESH)

    for h in range(HEADS):
        cols = slice(h * HS, (h + 1) * HS)
        state = lax.dot_general(
            k_ref[:, cols], v_ref[:, cols], (((0,), (0,)), ((), ())), preferred_element_type=F32
        )
        sq[cols, :] = state.astype(BF16)
    pl.semaphore_wait(barrier, len(peers))

    def quarter(i):
        return pl.ds(pl.multiple_of(i * 96, 96), 96)

    def send1(d):
        to = lax.rem(yl + d, 4)
        return remote(sq.at[quarter(to)], ra.at[yl], s1.at[d - 1], r1.at[d - 1], dev(yl=to))

    for d in (1, 2, 3):
        send1(d).start()
    ra[yl] = sq[quarter(yl), :]

    wt[z] = w_ref[...]
    w_ring = Ring(wt, lambda o: o, z, lambda way: dev(z=lax.rem(z + (1 if way == 0 else 7), 8)), ws, wr)

    w_ring.start()

    def recv1(d):
        frm = lax.rem(yl + 4 - d, 4)
        return remote(sq.at[quarter(yl)], ra.at[frm], s1.at[d - 1], r1.at[d - 1], dev(yl=frm))

    for d in (1, 2, 3):
        recv1(d).wait_recv()
    tot[...] = (
        (ra[0].astype(F32) + ra[1].astype(F32)) + (ra[2].astype(F32) + ra[3].astype(F32))
    ).astype(BF16)

    def copy2(d, to):
        return remote(tot, rb.at[d - 1], s2.at[d - 1], r2.at[d - 1], dev(z=to))

    for d in range(1, 8):
        @pl.when(z + d < 8)
        def _(d=d):
            copy2(d, lax.rem(z + d, 8)).start()

    rows = lax.broadcasted_iota(jnp.int32, (HS, HS), 0)
    columns = lax.broadcasted_iota(jnp.int32, (HS, HS), 1)
    for h in range(HEADS):
        cols = slice(h * HS, (h + 1) * HS)
        scores = jnp.where(rows >= columns, nt(q_ref[:, cols], k_ref[:, cols]), 0.0).astype(BF16)
        within[:, cols] = jnp.dot(scores, v_ref[:, cols], preferred_element_type=F32)

    w_ring.hop(1)
    base[...] = jnp.zeros_like(base)
    for d in range(1, 8):
        @pl.when(z >= d)
        def _(d=d):
            copy2(d, lax.rem(z + 8 - d, 8)).wait_recv()
            base[...] += rb[d - 1].astype(F32)
    running = base[...]
    for i in range(4):
        pfx[i] = running.astype(BF16)
        if i < 3:
            running = running + ra[i].astype(F32)

    def send3(d):
        to = lax.rem(yl + d, 4)
        return remote(pfx.at[to], rc.at[quarter(yl)], s3.at[d - 1], r3.at[d - 1], dev(yl=to))

    for d in (1, 2, 3):
        send3(d).start()
    rc[quarter(yl), :] = pfx[yl]

    w_ring.hop(2)

    def recv3(d):
        frm = lax.rem(yl + 4 - d, 4)
        return remote(pfx.at[yl], rc.at[quarter(frm)], s3.at[d - 1], r3.at[d - 1], dev(yl=frm))

    for d in (1, 2, 3):
        recv3(d).wait_recv()

    for h in range(HEADS):
        cols = slice(h * HS, (h + 1) * HS)
        mixed = within[:, cols] + jnp.dot(q_ref[:, cols], rc[cols, :], preferred_element_type=F32)
        scale = lax.rsqrt(jnp.mean(mixed * mixed, axis=-1, keepdims=True) + 1e-06)
        att[yl, :, cols] = (mixed * scale * g_ref[cols]).astype(BF16)

    def copy_a(d, to, frm):
        return remote(att.at[frm], att.at[frm], as_.at[d - 1], ar.at[d - 1], dev(yl=to))

    for d in (2, 1, 3):
        copy_a(d, lax.rem(yl + d, 4), yl).start()
    w_ring.hop(3)
    w_ring.hop(4)
    for d in (1, 2, 3):
        copy_a(d, lax.rem(yl + d, 4), lax.rem(yl + 4 - d, 4)).wait_recv()

    def tokens(half):
        return att[pl.ds(2 * half, 2)].reshape(2 * HS, HEADS * HS)

    def unit(e, i, a):
        return nt(wt[2 * lax.rem(x + i, 4) + lax.rem(yh + e, 2)], a)

    partner = dev(core=1 - core)

    def copy_c(e, i):
        n = e * 4 + i - 1
        return remote(pc_out.at[n], pc_in.at[n], cs.at[n], cr.at[n], partner)

    def copy_x(e, i, to):
        n = e * 3 + i - 1
        return remote(px_out.at[n], px_in.at[n], xs.at[n], xr.at[n], dev(x=to))

    theirs, ours = tokens(1 - core), tokens(core)

    def give(e, i):
        pc_out[e * 4 + i - 1] = unit(e, i, theirs).astype(BF16)
        copy_c(e, i).start()

    order = [(e, i) for e in (1, 0) for i in (1, 3, 2, 4)]
    give(*order[0])
    for n, (e, i) in enumerate(order):
        if n < 7:
            give(*order[n + 1])
        mine = unit(e, i, ours)
        copy_c(e, i).wait_recv()
        mine = mine + pc_in[e * 4 + i - 1].astype(F32)
        if i < 4:
            px_out[e * 3 + i - 1] = mine.astype(BF16)
            copy_x(e, i, lax.rem(x + i, 4)).start()
        else:
            f_acc[e] = mine

    half = lax.rem(yl, 2)

    def copy_f(e, i, slot):
        to = dev(yl=2 * core + i, yh=lax.rem(yh + e, 2), core=lax.div(yl, 2))
        return remote(f_out.at[e * 2 + i], f_in.at[e * 2 + slot], fs.at[e * 2 + i], fr.at[e * 2 + slot], to)

    def each_f(act, es=(1, 0)):
        for e in es:
            for i in (0, 1):
                if e:
                    act(e, i)
                else:
                    pl.when(2 * core + i != yl)(lambda e=e, i=i: act(e, i))

    for e in (1, 0):
        for i in (1, 2, 3):
            copy_x(e, i, lax.rem(x + 4 - i, 4)).wait_recv()
        total = f_acc[e]
        for i in (1, 2, 3):
            total = total + px_in[e * 3 + i - 1].astype(F32)
        f_out[e * 2] = total[:, :HS].astype(BF16)
        f_out[e * 2 + 1] = total[:, HS:].astype(BF16)
        each_f(lambda e, i: copy_f(e, i, half).start(), (e,))
    for i in (0, 1):
        @pl.when(2 * core + i == yl)
        def _(i=i):
            f_in[i] = f_out[i]
    each_f(lambda e, i: copy_f(e, i, i).wait_recv())

    same = f_in[0:2].reshape(HEADS * HS, HS).astype(F32)
    other = f_in[2:4].reshape(HEADS * HS, HS).astype(F32)
    o_ref[...] = jnp.transpose((same + other).astype(BF16))

    for d in (1, 2, 3):
        send1(d).wait_send()
        send3(d).wait_send()
        copy_x(0, d, lax.rem(x + d, 4)).wait_send()
        copy_x(1, d, lax.rem(x + d, 4)).wait_send()
    for d in range(1, 8):
        @pl.when(z + d < 8)
        def _(d=d):
            copy2(d, lax.rem(z + d, 8)).wait_send()

    w_ring.finish()
    for d in (1, 2, 3):
        copy_a(d, lax.rem(yl + d, 4), yl).wait_send()
    for i in (1, 2, 3, 4):
        copy_c(0, i).wait_send()
        copy_c(1, i).wait_send()
    each_f(lambda e, i: copy_f(e, i, half).wait_send())


def body(queries, keys, values, norm_gain, out_weight):
    dma = [pltpu.SemaphoreType.DMA((n,)) for n in (3, 7, 3, 16, 3, 8, 6, 4) for _ in (0, 1)]
    return pl.pallas_call(
        kernel,
        out_shape=jax.ShapeDtypeStruct((HS, HEADS * HS), BF16),
        in_specs=[pl.BlockSpec(memory_space=pltpu.VMEM)] * 5,
        out_specs=pl.BlockSpec(memory_space=pltpu.VMEM),
        scratch_shapes=[
            pltpu.VMEM((384, 128), BF16),
            pltpu.VMEM((4, 96, 128), BF16),
            pltpu.VMEM((96, 128), BF16),
            pltpu.VMEM((7, 96, 128), BF16),
            pltpu.VMEM((96, 128), F32),
            pltpu.VMEM((4, 96, 128), BF16),
            pltpu.VMEM((384, 128), BF16),
            pltpu.VMEM((128, 384), F32),
            pltpu.VMEM((4, 128, 384), BF16),
            pltpu.VMEM((8, 192, 384), BF16),
            pltpu.VMEM((8, 192, 256), BF16),
            pltpu.VMEM((8, 192, 256), BF16),
            pltpu.VMEM((6, 192, 256), BF16),
            pltpu.VMEM((6, 192, 256), BF16),
            pltpu.VMEM((2, 192, 256), F32),
            pltpu.VMEM((4, 192, 128), BF16),
            pltpu.VMEM((4, 192, 128), BF16),
        ] + dma,
        compiler_params=pltpu.CompilerParams(collective_id=0, has_side_effects=True),
    )(queries, keys, values, norm_gain, jnp.transpose(out_weight))


def solution(mesh):
    return jax.shard_map(
        body,
        mesh=mesh,
        in_specs=(P("ctx", "tp"), P("ctx", "tp"), P("ctx", "tp"), P("tp"), P("tp", "ctx")),
        out_specs=P("ctx", "tp"),
        check_vma=False,
    )
```
